32 devices in a mesh: parts: 2 (over y), tmpl: 4 (over z), sta: 4 (over x, core).
Axes of the slice: x: 2, y: 2, z: 4, core: 2. Of those that a mesh axis runs over, the one named last changes fastest.
Arguments:
- data: float32 [64, 3, 1280], P(('parts', 'sta'), None, 'tmpl'), parts along dimension 0, as said below
- templates: bfloat16 [32, 3, 16, 256], P('sta', None, 'tmpl'), as said below
- starts: int32 [32, 3, 16], P('sta', None, 'tmpl'), may hold values from 0 to 512
Outputs:
- network: float32 [32, 512], P(('parts', 'tmpl'), 'sta'), parts along dimension 0
The draws below stay inside these ranges and needn't reach their ends.
There are 2 independent parts, one for each index of `parts`. The reference program is written for one: setup_inputs(seed, part) draws one part's arguments, and reference() takes and returns one part's arrays. A program takes and returns all parts, laid end to end along the dimension named above; an argument that names none is the same for every part. Nothing has to cross between parts.
Inputs may be any that keep to these rules, and one draw needn't show every extreme that they name: `data`: finite samples. `templates`: finite samples.
All inputs are finite; a program needn't handle non-finite values.
Results may differ from the reference program's by a relative error of at most 0.0029.
Values sent between devices are 32-bit elements; how exact they have to be, the bound alone decides.
A program may use at most 64 MiB of HBM per device.

```python
import math
import jax
import jax.numpy as jnp
from jax import lax

TLEN = 256
MAXSHIFT = 512
LAGS = 512
TEMPLATES = 16
STATIONS = 32
SAMPLES = 1280


def draw_data(key, part):
    first_key, second_key = jax.random.split(key, 2)
    segments = (SAMPLES + 31) // 32
    levels = jax.random.uniform(second_key, (STATIONS, 3, segments), jnp.float32)
    random_part = jax.random.normal(first_key, (STATIONS, 3, SAMPLES), jnp.float32)
    envelope = jnp.exp(levels * math.log(10.0))
    envelope = jnp.repeat(envelope, 32, axis=2)[:, :, :SAMPLES]
    return (random_part * envelope).astype(jnp.float32)


def draw_templates(key, part):
    first_key, second_key, third_key = jax.random.split(key, 3)
    segments = (TLEN + 7) // 8
    random_part = jax.random.normal(first_key, (STATIONS, 3, TEMPLATES, TLEN), jnp.float32)
    row_scale = jnp.exp(jax.random.uniform(second_key, (STATIONS, 3, TEMPLATES, 1), jnp.float32) * math.log(10.0)) * 0.1
    levels = jax.random.uniform(third_key, (STATIONS, 3, TEMPLATES, segments), jnp.float32)
    envelope = jnp.repeat(jnp.exp(levels * math.log(3.0)), 8, axis=3)[:, :, :, :TLEN]
    return (random_part * row_scale * envelope).astype(jnp.bfloat16)


def with_ends(result, key, least, high):
    longest = result.shape.index(max(result.shape))
    spots = []
    for shift in (0, 1):
        where = [jax.random.randint(jax.random.fold_in(key, axis), (), 0, length) for axis, length in enumerate(result.shape)]
        where[longest] = (where[longest] + shift) % result.shape[longest]
        spots.append(tuple(where))
    return result.at[spots[0]].set(least).at[spots[1]].set(high)


def setup_inputs(seed: int = 0, part: int = 0) -> dict:
    streams_of = jax.random.split(jax.random.key(seed), 4)
    own_keys = jax.random.split(jax.random.fold_in(streams_of[3], part), 4)
    return {
        "data": draw_data(jax.random.fold_in(jax.random.fold_in(streams_of[3], part), 71), part),
        "templates": draw_templates(jax.random.fold_in(streams_of[3], 71), part),
        "starts": with_ends(jax.random.randint(streams_of[2], (STATIONS, 3, TEMPLATES), 0, MAXSHIFT + 1), jax.random.fold_in(streams_of[2], 1), 0, MAXSHIFT).astype(jnp.int32),
    }


EPS = 1e-06

def window_energy(trace):
    extent = LAGS + MAXSHIFT
    squares = trace * trace
    running = jnp.concatenate([jnp.zeros_like(squares[:, :1]), jnp.cumsum(squares, axis=1)], axis=1)
    return running[:, TLEN:TLEN + extent] - running[:, :extent]

def station_term(trace, waves, offsets):
    extent = LAGS + MAXSHIFT
    lowered = lax.optimization_barrier(trace.astype(jnp.bfloat16)).astype(jnp.float32)
    kernel = waves.astype(jnp.float32).reshape(-1, 1, waves.shape[-1])
    raw = lax.conv_general_dilated(lowered[None], kernel, (1,), 'VALID', dimension_numbers=('NCH', 'OIH', 'NCH'), feature_group_count=3, precision=lax.Precision.HIGHEST, preferred_element_type=jnp.float32)[0]
    raw = raw.reshape(3, waves.shape[1], -1)[:, :, :extent]
    energy = window_energy(trace)
    tnorm = lax.optimization_barrier(jnp.sum(waves.astype(jnp.float32) ** 2, axis=-1))
    index = offsets.astype(jnp.int32)[:, :, None] + jnp.arange(LAGS, dtype=jnp.int32)[None, None, :]
    aligned = jnp.take_along_axis(raw, index, axis=2)
    channel = jnp.arange(3, dtype=jnp.int32)[:, None, None]
    local = energy[channel, index]
    scale = TLEN * jnp.sqrt((tnorm[:, :, None] / TLEN + EPS) * (local / TLEN + EPS))
    return lax.optimization_barrier(jnp.sum(aligned / scale, axis=0))

def reference(data, templates, starts):

    def step(total, items):
        trace, waves, offsets = items
        return (total + station_term(trace, waves, offsets), None)
    start_total = jnp.zeros((templates.shape[2], LAGS), jnp.float32)
    total, _ = lax.scan(step, start_total, (data, templates, starts))
    return total
```

```python
import functools

import jax
import jax.numpy as jnp
from jax import lax
from jax.experimental import pallas as pl
from jax.experimental.pallas import tpu as pltpu
from jax.sharding import PartitionSpec as P

TLEN = 256
MAXSHIFT = 512
LAGS = 512
EXTENT = LAGS + MAXSHIFT
LANE = 128
CHUNKS = EXTENT // LANE
HALF = LANE // 2
BAND = TLEN + LANE
ROWS = 16
EPS = 1e-06

MESH = pl.DeviceIdType.MESH


def kernel(
    peers, owners,
    starts_hbm, data_ref, templates_hbm, out_ref,
    starts_ref, templates_ref, local_sems, gathered, chunked, flat, bands, norms, inverse, lagged, partial_ref, arrived,
    turns, chunks,
    data_send, data_recv, sum_send, sum_recv, ready, columns, go,
):
    channels, stations, width = data_ref.shape
    per_group = templates_ref.shape[2]
    groups = stations * channels
    samples = width * peers
    my_tmpl = lax.axis_index("tmpl")
    my_sta = lax.axis_index("sta")

    fetches = [
        pltpu.make_async_copy(templates_hbm, templates_ref, local_sems.at[0]),
        pltpu.make_async_copy(starts_hbm, starts_ref, local_sems.at[1]),
        pltpu.make_async_copy(data_ref, gathered.at[my_tmpl], local_sems.at[2]),
    ]
    for copy in fetches:
        copy.start()

    barrier = pltpu.get_barrier_semaphore()
    for step in range(1, peers):
        @pl.when(my_tmpl + step < peers)
        def _():
            pl.semaphore_signal(barrier, inc=1, device_id={"tmpl": my_tmpl + step}, device_id_type=MESH)
    @pl.when(my_tmpl == 0)
    def _():
        for step in range(1, owners):
            pl.semaphore_signal(
                barrier, inc=1, device_id={"sta": lax.rem(my_sta + step, owners)}, device_id_type=MESH
            )
    @pl.when(my_tmpl > 0)
    def _():
        pl.semaphore_wait(barrier, my_tmpl)

    def block_to(target, source):
        return pltpu.make_async_remote_copy(
            src_ref=source,
            dst_ref=gathered.at[my_tmpl],
            send_sem=data_send.at[target],
            recv_sem=data_recv.at[my_tmpl],
            device_id={"tmpl": target},
            device_id_type=MESH,
        )

    for target in range(peers - 1):
        @pl.when(target < my_tmpl)
        def _():
            pl.semaphore_signal(ready.at[my_tmpl], inc=1, device_id={"tmpl": target}, device_id_type=MESH)
            block_to(target, data_ref).start()

    def prepare():
        fetches[0].wait()
        fetches[1].wait()
        for s in range(stations):
            for c in range(channels):
                row = (s * channels + c) * per_group
                flat[row : row + per_group, :] = templates_ref[s, c].astype(jnp.float32)
        waves = flat[...]
        tnorm = jnp.sum(waves * waves, axis=1, keepdims=True)
        norms[...] = jnp.broadcast_to(lax.rsqrt(tnorm / TLEN + EPS) / TLEN, norms.shape)
        down = lax.broadcasted_iota(jnp.int32, (TLEN, TLEN), 0)
        across = lax.broadcasted_iota(jnp.int32, (TLEN, TLEN), 1)
        flip = jnp.where(down + across == TLEN - 1, 1.0, 0.0).astype(jnp.bfloat16)
        flat[...] = jnp.dot(waves.astype(jnp.bfloat16), flip, preferred_element_type=jnp.float32)
        for row in range(groups * per_group):
            s, c, t = row // (channels * per_group), row // per_group % channels, row % per_group
            start = starts_ref[c, t, s]
            turns[row] = (0 - start) & (LANE - 1)
            chunks[row] = (start + LANE - 1) >> 7

    sub = lax.broadcasted_iota(jnp.int32, (8, LANE), 0)
    lane = lax.broadcasted_iota(jnp.int32, (8, LANE), 1)

    left = lane < HALF

    def build(step, carry):
        for pair in range(4 * per_group // 2):
            group, pair = step * 4 + pair // (per_group // 2), pair % (per_group // 2)
            rows = []
            for k in range(2):
                row = flat[pl.ds(group * per_group + 2 * pair + k, 1), :]
                rows.append(
                    [jnp.broadcast_to(row[:, LANE:], (8, LANE)), jnp.broadcast_to(row[:, :LANE], (8, LANE))]
                )
            for block in range(HALF // 16):
                parts = [[], [], [], [], []]
                for q in (2 * block, 2 * block + 1):
                    keep = (lane & (HALF - 1)) <= sub + 8 * q
                    near = [
                        [pltpu.roll(x, 8 * q + 1, 1, stride=1, stride_axis=0) for x in row] for row in rows
                    ]
                    far = [
                        [pltpu.roll(x, 8 * q + 1 + HALF, 1, stride=1, stride_axis=0) for x in row]
                        for row in rows
                    ]
                    low, high = [jnp.where(left, near[0][i], far[1][i]) for i in range(2)]
                    parts[0].append(jnp.where(keep, low, 0.0))
                    parts[2].append(jnp.where(keep, high, low))
                    parts[4].append(jnp.where(keep, 0.0, high))
                    parts[1].append(jnp.where(left, far[0][0], near[1][0]))
                    parts[3].append(jnp.where(left, far[0][1], near[1][1]))
                for k in range(5):
                    top = k * HALF + block * 16
                    bands[group, top : top + 16, pair * LANE : (pair + 1) * LANE] = jnp.concatenate(
                        parts[k], axis=0
                    ).astype(jnp.bfloat16)
        return carry

    steps = groups // 4
    early = jnp.where(my_tmpl == 0, steps, jnp.where(my_tmpl * 2 < peers, steps // 2, 0))
    ahead = my_tmpl * 2 < peers
    pl.when(ahead)(prepare)
    lax.fori_loop(0, early, build, 0)

    fetches[2].wait()
    for target in range(1, peers):
        @pl.when(target > my_tmpl)
        def _():
            pl.semaphore_wait(ready.at[target], 1)
            block_to(target, gathered.at[my_tmpl]).start()

    @pl.when(my_tmpl == 0)
    def _():
        pl.semaphore_wait(barrier, owners - 1)
        for step in range(1, owners):
            pl.semaphore_signal(
                columns, inc=1, device_id={"sta": lax.rem(my_sta + step, owners)}, device_id_type=MESH
            )
        pl.semaphore_wait(columns, owners - 1)
        for target in range(1, peers):
            pl.semaphore_signal(go, inc=1, device_id={"tmpl": target}, device_id_type=MESH)

    pl.when(jnp.logical_not(ahead))(prepare)
    lax.fori_loop(early, steps, build, 0)

    for step in range(1, peers):
        source = lax.rem(my_tmpl + peers - step, peers)
        pltpu.make_async_remote_copy(
            src_ref=data_ref,
            dst_ref=gathered.at[source],
            send_sem=data_send.at[step],
            recv_sem=data_recv.at[source],
            device_id={"tmpl": source},
            device_id_type=MESH,
        ).wait_recv()
    for c in range(channels):
        whole = jnp.concatenate([gathered[i, c] for i in range(peers)], axis=1)
        later = jnp.concatenate([whole[:, HALF:], whole[:, :HALF]], axis=1)
        for j in range(samples // LANE):
            rows = pl.ds(c * ROWS + j, stations, stride=channels * ROWS)
            chunked[0, rows, :] = whole[:, j * LANE : (j + 1) * LANE]
            chunked[1, rows, :] = later[:, j * LANE : (j + 1) * LANE]

    def windows(which, group):
        return jnp.concatenate(
            [chunked[which, group * ROWS + i : group * ROWS + i + CHUNKS, :] for i in range(3)], axis=1
        )

    squares = []
    for group in range(groups):
        samples_in = windows(0, group)
        squares.append(samples_in * samples_in)
    squares = jnp.concatenate(squares, axis=0).astype(jnp.bfloat16)
    offset = lax.broadcasted_iota(jnp.int32, (BAND, LANE), 0) - lax.broadcasted_iota(
        jnp.int32, (BAND, LANE), 1
    )
    ones = jnp.where((offset >= 0) & (offset < TLEN), 1.0, 0.0).astype(jnp.bfloat16)
    energy = jnp.dot(squares, ones, preferred_element_type=jnp.float32)
    inverse[...] = lax.rsqrt(energy / TLEN + EPS)

    for group in range(groups):
        both = jnp.concatenate([windows(0, group), windows(1, group)], axis=0).astype(jnp.bfloat16)
        raw = jnp.dot(both[:, : TLEN + HALF], bands[group], preferred_element_type=jnp.float32)
        local = inverse[group * CHUNKS : (group + 1) * CHUNKS, :]
        for pair in range(per_group // 2):
            even = raw[:CHUNKS, pair * LANE : (pair + 1) * LANE]
            odd = raw[CHUNKS:, pair * LANE : (pair + 1) * LANE]
            for k, value in enumerate((
                jnp.where(left, even, pltpu.roll(odd, HALF, 1)),
                jnp.where(left, pltpu.roll(even, HALF, 1), odd),
            )):
                row = group * per_group + 2 * pair + k
                lagged[row, 1 : CHUNKS + 1, :] = value * (local * norms[row : row + 1, :])

    zero = jnp.zeros((CHUNKS, LANE), jnp.float32)
    for t in range(per_group):
        same, following = zero, zero
        for group in range(groups):
            row = group * per_group + t
            turn = turns[row]
            moved = pltpu.roll(lagged[row, pl.ds(chunks[row], CHUNKS), :], turn, 1)
            keep = lane < turn
            same = same + jnp.where(keep, moved, 0.0)
            following = following + jnp.where(keep, 0.0, moved)
        rows = LAGS // LANE
        partial_ref[:, t, :] = same[:rows] + following[1 : rows + 1]

    span = LAGS // LANE // owners
    @pl.when(my_tmpl > 0)
    def _():
        pl.semaphore_wait(go, 1)
    sends = []
    for step in range(owners - 1):
        target = step + jnp.where(my_sta <= step, 1, 0)
        copy = pltpu.make_async_remote_copy(
            src_ref=partial_ref.at[pl.ds(target * span, span)],
            dst_ref=arrived.at[my_sta],
            send_sem=sum_send.at[step],
            recv_sem=sum_recv.at[my_sta],
            device_id={"sta": target},
            device_id_type=MESH,
        )
        copy.start()
        sends.append(copy)
    total = partial_ref[pl.ds(my_sta * span, span)]
    for step in range(1, owners):
        source = lax.rem(my_sta + owners - step, owners)
        pltpu.make_async_remote_copy(
            src_ref=partial_ref.at[pl.ds(source * span, span)],
            dst_ref=arrived.at[source],
            send_sem=sum_send.at[step],
            recv_sem=sum_recv.at[source],
            device_id={"sta": source},
            device_id_type=MESH,
        ).wait_recv()
        total = total + arrived[source]
    for i in range(span):
        out_ref[:, i * LANE : (i + 1) * LANE] = total[i]
    for copy in sends:
        copy.wait_send()
    for step in range(1, peers):
        block_to(lax.rem(my_tmpl + step, peers), data_ref).wait_send()


def shards(data, templates, starts):
    peers, owners = lax.axis_size("tmpl"), lax.axis_size("sta")
    stations, channels, width = data.shape
    per_group = templates.shape[2]
    groups = stations * channels
    vmem = pl.BlockSpec(memory_space=pltpu.VMEM)
    span = LAGS // LANE // owners
    return pl.pallas_call(
        functools.partial(kernel, peers, owners),
        out_shape=jax.ShapeDtypeStruct((per_group, LAGS // owners), jnp.float32),
        in_specs=[pl.BlockSpec(memory_space=pltpu.HBM)] * 3,
        out_specs=vmem,
        scratch_shapes=[
            pltpu.SMEM((channels, per_group, stations), jnp.int32),
            pltpu.VMEM(templates.shape, templates.dtype),
            pltpu.SemaphoreType.DMA((3,)),
            pltpu.VMEM((peers, channels, stations, width), jnp.float32),
            pltpu.VMEM((2, groups * ROWS, LANE), jnp.float32),
            pltpu.VMEM((groups * per_group, TLEN), jnp.float32),
            pltpu.VMEM((groups, TLEN + HALF, per_group * HALF), jnp.bfloat16),
            pltpu.VMEM((groups * per_group, LANE), jnp.float32),
            pltpu.VMEM((groups * CHUNKS, LANE), jnp.float32),
            pltpu.VMEM((groups * per_group, ROWS, LANE), jnp.float32),
            pltpu.VMEM((LAGS // LANE, per_group, LANE), jnp.float32),
            pltpu.VMEM((owners, span, per_group, LANE), jnp.float32),
            pltpu.SMEM((groups * per_group,), jnp.int32),
            pltpu.SMEM((groups * per_group,), jnp.int32),
            pltpu.SemaphoreType.DMA((peers,)),
            pltpu.SemaphoreType.DMA((peers,)),
            pltpu.SemaphoreType.DMA((owners,)),
            pltpu.SemaphoreType.DMA((owners,)),
            pltpu.SemaphoreType.REGULAR((peers,)),
            pltpu.SemaphoreType.REGULAR,
            pltpu.SemaphoreType.REGULAR,
        ],
        compiler_params=pltpu.CompilerParams(
            collective_id=0, has_side_effects=True, vmem_limit_bytes=64 * 1024 * 1024 - 10559488
        ),
    )(jnp.transpose(starts, (1, 2, 0)), jnp.transpose(data, (1, 0, 2)), templates)


def solution(mesh):
    return jax.shard_map(
        shards,
        mesh=mesh,
        in_specs=(
            P(("parts", "sta"), None, "tmpl"),
            P("sta", None, "tmpl", None),
            P("sta", None, "tmpl"),
        ),
        out_specs=P(("parts", "tmpl"), "sta"),
        check_vma=False,
    )
```

```python
import functools

import jax
import jax.numpy as jnp
from jax import lax
from jax.experimental import pallas as pl
from jax.experimental.pallas import tpu as pltpu
from jax.sharding import PartitionSpec as P

TLEN = 256
MAXSHIFT = 512
LAGS = 512
EXTENT = LAGS + MAXSHIFT
LANE = 128
CHUNKS = EXTENT // LANE
HALF = LANE // 2
BAND = TLEN + LANE
ROWS = 16
EPS = 1e-06

MESH = pl.DeviceIdType.MESH


def kernel(
    peers, owners,
    starts_hbm, data_ref, templates_hbm, out_ref,
    starts_ref, templates_ref, local_sems, gathered, chunked, flat, bands, norms, inverse, lagged, partial_ref, arrived,
    turns, chunks,
    data_recv, send_sem, sum_recv, ready, relay,
):
    channels, stations, width = data_ref.shape
    per_group = templates_ref.shape[2]
    groups = stations * channels
    samples = width * peers
    my_tmpl = lax.axis_index("tmpl")
    my_sta = lax.axis_index("sta")

    last = my_tmpl == peers - 1
    barrier = pltpu.get_barrier_semaphore()

    def block_to(target):
        return pltpu.make_async_remote_copy(
            src_ref=data_ref,
            dst_ref=gathered.at[my_tmpl],
            send_sem=send_sem,
            recv_sem=data_recv,
            device_id={"tmpl": target},
            device_id_type=MESH,
        )

    @pl.when(last)
    def _():
        pl.semaphore_wait(barrier, peers - 1)
        for target in range(peers - 1):
            block_to(target).start()
            pl.semaphore_signal(ready.at[peers - 2], inc=1, device_id={"tmpl": target}, device_id_type=MESH)

    fetches = [
        pltpu.make_async_copy(templates_hbm, templates_ref, local_sems.at[0]),
        pltpu.make_async_copy(starts_hbm, starts_ref, local_sems.at[1]),
        pltpu.make_async_copy(data_ref, gathered.at[my_tmpl], data_recv),
    ]
    for copy in fetches:
        copy.start()

    @pl.when(jnp.logical_not(last))
    def _():
        for step in range(1, peers):
            @pl.when(my_tmpl + step < peers)
            def _():
                pl.semaphore_signal(
                    barrier, inc=1, device_id={"tmpl": my_tmpl + step}, device_id_type=MESH
                )

        @pl.when(my_tmpl == 0)
        def _():
            for step in range(1, owners):
                pl.semaphore_signal(
                    barrier, inc=1, device_id={"sta": lax.rem(my_sta + step, owners)}, device_id_type=MESH
                )

        @pl.when(my_tmpl > 0)
        def _():
            pl.semaphore_wait(barrier, my_tmpl)
            for target in range(peers - 2):
                @pl.when(target < my_tmpl)
                def _():
                    block_to(target).start()
                    pl.semaphore_signal(
                        ready.at[my_tmpl - 1], inc=1, device_id={"tmpl": target}, device_id_type=MESH
                    )

    def prepare():
        fetches[0].wait()
        fetches[1].wait()
        for s in range(stations):
            for c in range(channels):
                row = (s * channels + c) * per_group
                flat[row : row + per_group, :] = templates_ref[s, c].astype(jnp.float32)
        waves = flat[...]
        tnorm = jnp.sum(waves * waves, axis=1, keepdims=True)
        norms[...] = jnp.broadcast_to(lax.rsqrt(tnorm / TLEN + EPS) / TLEN, norms.shape)
        down = lax.broadcasted_iota(jnp.int32, (TLEN, TLEN), 0)
        across = lax.broadcasted_iota(jnp.int32, (TLEN, TLEN), 1)
        flip = jnp.where(down + across == TLEN - 1, 1.0, 0.0).astype(jnp.bfloat16)
        flat[...] = jnp.dot(waves.astype(jnp.bfloat16), flip, preferred_element_type=jnp.float32)
        for row in range(groups * per_group):
            s, c, t = row // (channels * per_group), row // per_group % channels, row % per_group
            start = starts_ref[c, t, s]
            turns[row] = (0 - start) & (LANE - 1)
            chunks[row] = (start + LANE - 1) >> 7

    sub = lax.broadcasted_iota(jnp.int32, (8, LANE), 0)
    lane = lax.broadcasted_iota(jnp.int32, (8, LANE), 1)

    left = lane < HALF

    def build(step, carry):
        for pair in range(4 * per_group // 2):
            group, pair = step * 4 + pair // (per_group // 2), pair % (per_group // 2)
            rows = []
            for k in range(2):
                row = flat[pl.ds(group * per_group + 2 * pair + k, 1), :]
                rows.append(
                    [jnp.broadcast_to(row[:, LANE:], (8, LANE)), jnp.broadcast_to(row[:, :LANE], (8, LANE))]
                )
            for block in range(HALF // 16):
                parts = [[], [], [], [], []]
                for q in (2 * block, 2 * block + 1):
                    keep = (lane & (HALF - 1)) <= sub + 8 * q
                    near = [
                        [pltpu.roll(x, 8 * q + 1, 1, stride=1, stride_axis=0) for x in row] for row in rows
                    ]
                    far = [
                        [pltpu.roll(x, 8 * q + 1 + HALF, 1, stride=1, stride_axis=0) for x in row]
                        for row in rows
                    ]
                    low, high = [jnp.where(left, near[0][i], far[1][i]) for i in range(2)]
                    parts[0].append(jnp.where(keep, low, 0.0))
                    parts[2].append(jnp.where(keep, high, low))
                    parts[4].append(jnp.where(keep, 0.0, high))
                    parts[1].append(jnp.where(left, far[0][0], near[1][0]))
                    parts[3].append(jnp.where(left, far[0][1], near[1][1]))
                for k in range(5):
                    top = k * HALF + block * 16
                    bands[group, top : top + 16, pair * LANE : (pair + 1) * LANE] = jnp.concatenate(
                        parts[k], axis=0
                    ).astype(jnp.bfloat16)
        return carry

    steps = groups // 4
    early = jnp.where(my_tmpl == 0, steps, jnp.where(my_tmpl * 2 < peers, steps // 2, 0))
    ahead = my_tmpl * 2 < peers
    pl.when(ahead)(prepare)
    lax.fori_loop(0, early, build, 0)

    for target in range(1, peers):
        @pl.when(target > my_tmpl)
        def _():
            pl.semaphore_wait(ready.at[target - 1], 1)
            block_to(target).start()

    @pl.when(my_tmpl == 0)
    def _():
        pl.semaphore_wait(barrier, owners - 1)
        for step in range(1, owners):
            pl.semaphore_signal(
                relay, inc=1, device_id={"sta": lax.rem(my_sta + step, owners)}, device_id_type=MESH
            )
        pl.semaphore_wait(relay, owners - 1)
        for target in range(1, peers):
            pl.semaphore_signal(relay, inc=1, device_id={"tmpl": target}, device_id_type=MESH)

    pl.when(jnp.logical_not(ahead))(prepare)
    lax.fori_loop(early, steps, build, 0)

    pltpu.make_async_copy(gathered, gathered, data_recv).wait()
    for c in range(channels):
        whole = jnp.concatenate([gathered[i, c] for i in range(peers)], axis=1)
        later = jnp.concatenate([whole[:, HALF:], whole[:, :HALF]], axis=1)
        for j in range(samples // LANE):
            rows = pl.ds(c * ROWS + j, stations, stride=channels * ROWS)
            chunked[0, rows, :] = whole[:, j * LANE : (j + 1) * LANE]
            chunked[1, rows, :] = later[:, j * LANE : (j + 1) * LANE]

    def windows(which, group):
        return jnp.concatenate(
            [chunked[which, group * ROWS + i : group * ROWS + i + CHUNKS, :] for i in range(3)], axis=1
        )

    squares = []
    for group in range(groups):
        samples_in = windows(0, group)
        squares.append(samples_in * samples_in)
    squares = jnp.concatenate(squares, axis=0).astype(jnp.bfloat16)
    offset = lax.broadcasted_iota(jnp.int32, (BAND, LANE), 0) - lax.broadcasted_iota(
        jnp.int32, (BAND, LANE), 1
    )
    ones = jnp.where((offset >= 0) & (offset < TLEN), 1.0, 0.0).astype(jnp.bfloat16)
    energy = jnp.dot(squares, ones, preferred_element_type=jnp.float32)
    inverse[...] = lax.rsqrt(energy / TLEN + EPS)

    def correlate(group):
        both = jnp.concatenate([windows(0, group), windows(1, group)], axis=0).astype(jnp.bfloat16)
        raw = jnp.dot(both[:, : TLEN + HALF], bands[group], preferred_element_type=jnp.float32)
        local = inverse[group * CHUNKS : (group + 1) * CHUNKS, :]
        for pair in range(per_group // 2):
            even = raw[:CHUNKS, pair * LANE : (pair + 1) * LANE]
            odd = raw[CHUNKS:, pair * LANE : (pair + 1) * LANE]
            for k, value in enumerate((
                jnp.where(left, even, pltpu.roll(odd, HALF, 1)),
                jnp.where(left, pltpu.roll(even, HALF, 1), odd),
            )):
                row = group * per_group + 2 * pair + k
                lagged[row, 1 : CHUNKS + 1, :] = value * (local * norms[row : row + 1, :])

    zero = jnp.zeros((CHUNKS, LANE), jnp.float32)
    same, following = [zero] * per_group, [zero] * per_group

    def align(group):
        for t in range(per_group):
            row = group * per_group + t
            turn = turns[row]
            moved = pltpu.roll(lagged[row, pl.ds(chunks[row], CHUNKS), :], turn, 1)
            keep = lane < turn
            same[t] = same[t] + jnp.where(keep, moved, 0.0)
            following[t] = following[t] + jnp.where(keep, 0.0, moved)

    behind = 0
    for group in range(groups + behind):
        if group < groups:
            correlate(group)
        if group >= behind:
            align(group - behind)
    rows = LAGS // LANE
    for t in range(per_group):
        partial_ref[:, t, :] = same[t][:rows] + following[t][1 : rows + 1]

    span = LAGS // LANE // owners
    @pl.when(my_tmpl > 0)
    def _():
        pl.semaphore_wait(relay, 1)
    others = gathered.at[pl.ds(0, peers - 1)]
    pltpu.make_async_copy(others, others, send_sem).wait()
    for step in range(owners - 1):
        target = step + jnp.where(my_sta <= step, 1, 0)
        pltpu.make_async_remote_copy(
            src_ref=partial_ref.at[pl.ds(target * span, span)],
            dst_ref=arrived.at[lax.rem(my_sta + owners - target, owners) - 1],
            send_sem=send_sem,
            recv_sem=sum_recv,
            device_id={"sta": target},
            device_id_type=MESH,
        ).start()
    total = partial_ref[pl.ds(my_sta * span, span)]
    pltpu.make_async_copy(arrived, arrived, sum_recv).wait()
    for step in range(owners - 1):
        total = total + arrived[step]
    for i in range(span):
        out_ref[:, i * LANE : (i + 1) * LANE] = total[i]
    pltpu.make_async_copy(arrived, arrived, send_sem).wait()


def shards(data, templates, starts):
    peers, owners = lax.axis_size("tmpl"), lax.axis_size("sta")
    stations, channels, width = data.shape
    per_group = templates.shape[2]
    groups = stations * channels
    vmem = pl.BlockSpec(memory_space=pltpu.VMEM)
    span = LAGS // LANE // owners
    return pl.pallas_call(
        functools.partial(kernel, peers, owners),
        out_shape=jax.ShapeDtypeStruct((per_group, LAGS // owners), jnp.float32),
        in_specs=[pl.BlockSpec(memory_space=pltpu.HBM)] * 3,
        out_specs=vmem,
        scratch_shapes=[
            pltpu.SMEM((channels, per_group, stations), jnp.int32),
            pltpu.VMEM(templates.shape, templates.dtype),
            pltpu.SemaphoreType.DMA((2,)),
            pltpu.VMEM((peers, channels, stations, width), jnp.float32),
            pltpu.VMEM((2, groups * ROWS, LANE), jnp.float32),
            pltpu.VMEM((groups * per_group, TLEN), jnp.float32),
            pltpu.VMEM((groups, TLEN + HALF, per_group * HALF), jnp.bfloat16),
            pltpu.VMEM((groups * per_group, LANE), jnp.float32),
            pltpu.VMEM((groups * CHUNKS, LANE), jnp.float32),
            pltpu.VMEM((groups * per_group, ROWS, LANE), jnp.float32),
            pltpu.VMEM((LAGS // LANE, per_group, LANE), jnp.float32),
            pltpu.VMEM((owners - 1, span, per_group, LANE), jnp.float32),
            pltpu.SMEM((groups * per_group,), jnp.int32),
            pltpu.SMEM((groups * per_group,), jnp.int32),
            pltpu.SemaphoreType.DMA,
            pltpu.SemaphoreType.DMA,
            pltpu.SemaphoreType.DMA,
            pltpu.SemaphoreType.REGULAR((peers - 1,)),
            pltpu.SemaphoreType.REGULAR,
        ],
        compiler_params=pltpu.CompilerParams(
            collective_id=0, has_side_effects=True, vmem_limit_bytes=64 * 1024 * 1024 - 10559488
        ),
    )(jnp.transpose(starts, (1, 2, 0)), jnp.transpose(data, (1, 0, 2)), templates)


def solution(mesh):
    return jax.shard_map(
        shards,
        mesh=mesh,
        in_specs=(
            P(("parts", "sta"), None, "tmpl"),
            P("sta", None, "tmpl", None),
            P("sta", None, "tmpl"),
        ),
        out_specs=P(("parts", "tmpl"), "sta"),
        check_vma=False,
    )
```

```python
import functools

import jax
import jax.numpy as jnp
from jax import lax
from jax.experimental import pallas as pl
from jax.experimental.pallas import tpu as pltpu
from jax.sharding import PartitionSpec as P

TLEN = 256
MAXSHIFT = 512
LAGS = 512
EXTENT = LAGS + MAXSHIFT
LANE = 128
CHUNKS = EXTENT // LANE
HALF = LANE // 2
QUARTER = LANE // 4
BAND = TLEN + LANE
ROWS = 16
EPS = 1e-06

MESH = pl.DeviceIdType.MESH


def kernel(
    peers, owners,
    starts_hbm, data_ref, templates_hbm, out_ref,
    starts_ref, templates_ref, local_sems, gathered, chunked, flat, bands, norms, inverse, lagged, partial_ref, arrived,
    turns, chunks,
    data_recv, send_sem, sum_sent, sum_recv, ready, relay,
):
    channels, stations, width = data_ref.shape
    per_group = templates_ref.shape[2]
    groups = stations * channels
    samples = width * peers
    my_tmpl = lax.axis_index("tmpl")
    my_sta = lax.axis_index("sta")

    last = my_tmpl == peers - 1
    patient = lax.rem(my_sta, 2) == 1
    barrier = pltpu.get_barrier_semaphore()

    def block_to(target):
        return pltpu.make_async_remote_copy(
            src_ref=data_ref,
            dst_ref=gathered.at[my_tmpl],
            send_sem=send_sem,
            recv_sem=data_recv,
            device_id={"tmpl": target},
            device_id_type=MESH,
        )

    @pl.when(last)
    def _():
        pl.semaphore_wait(barrier, peers - 1)
        block_to(0).start()
        for target in range(peers - 1):
            pl.semaphore_signal(ready.at[peers - 2], inc=1, device_id={"tmpl": target}, device_id_type=MESH)

        @pl.when(jnp.logical_not(patient))
        def _():
            for target in range(1, peers - 1):
                block_to(target).start()

    fetches = [
        pltpu.make_async_copy(templates_hbm, templates_ref, local_sems.at[0]),
        pltpu.make_async_copy(starts_hbm, starts_ref, local_sems.at[1]),
        pltpu.make_async_copy(data_ref, gathered.at[my_tmpl], data_recv),
    ]
    for copy in fetches:
        copy.start()

    @pl.when(jnp.logical_not(last))
    def _():
        for step in range(1, peers):
            @pl.when(my_tmpl + step < peers)
            def _():
                pl.semaphore_signal(
                    barrier, inc=1, device_id={"tmpl": my_tmpl + step}, device_id_type=MESH
                )

        @pl.when(my_tmpl == 0)
        def _():
            for step in range(1, owners):
                pl.semaphore_signal(
                    barrier, inc=1, device_id={"sta": lax.rem(my_sta + step, owners)}, device_id_type=MESH
                )

        @pl.when(my_tmpl > 0)
        def _():
            pl.semaphore_wait(barrier, my_tmpl)
            for target in range(peers - 2):
                @pl.when(target < my_tmpl)
                def _():
                    block_to(target).start()
                    pl.semaphore_signal(
                        ready.at[my_tmpl - 1], inc=1, device_id={"tmpl": target}, device_id_type=MESH
                    )

    def prepare():
        fetches[0].wait()
        fetches[1].wait()
        for s in range(stations):
            for c in range(channels):
                row = (s * channels + c) * per_group
                flat[row : row + per_group, :] = templates_ref[s, c].astype(jnp.float32)
        waves = flat[...]
        tnorm = jnp.sum(waves * waves, axis=1, keepdims=True)
        norms[...] = jnp.broadcast_to(lax.rsqrt(tnorm / TLEN + EPS) / TLEN, norms.shape)
        down = lax.broadcasted_iota(jnp.int32, (TLEN, TLEN), 0)
        across = lax.broadcasted_iota(jnp.int32, (TLEN, TLEN), 1)
        flip = jnp.where(down + across == TLEN - 1, 1.0, 0.0).astype(jnp.bfloat16)
        flat[...] = jnp.dot(waves.astype(jnp.bfloat16), flip, preferred_element_type=jnp.float32)
        for row in range(groups * per_group):
            s, c, t = row // (channels * per_group), row // per_group % channels, row % per_group
            start = starts_ref[c, t, s]
            turns[row] = (0 - start) & (LANE - 1)
            chunks[row] = (start + LANE - 1) >> 7

    sub = lax.broadcasted_iota(jnp.int32, (8, LANE), 0)
    lane = lax.broadcasted_iota(jnp.int32, (8, LANE), 1)

    left = lane < HALF
    even_quarter = (lane & QUARTER) == 0

    def build(step, carry):
        for quad in range(per_group):
            group, quad = step * 4 + quad // (per_group // 4), quad % (per_group // 4)
            rows = []
            for k in range(4):
                row = flat[pl.ds(group * per_group + 4 * quad + k, 1), :]
                rows.append(
                    [jnp.broadcast_to(row[:, LANE:], (8, LANE)), jnp.broadcast_to(row[:, :LANE], (8, LANE))]
                )
            for block in range(LANE // 16):
                parts = {}
                for q in (2 * block, 2 * block + 1):
                    turned = [
                        [
                            pltpu.roll(x, (8 * q + QUARTER * k + 1) % LANE, 1, stride=1, stride_axis=0)
                            for x in rows[k]
                        ]
                        for k in range(4)
                    ]
                    low, high = [
                        jnp.where(
                            left,
                            jnp.where(even_quarter, turned[0][i], turned[1][i]),
                            jnp.where(even_quarter, turned[2][i], turned[3][i]),
                        )
                        for i in range(2)
                    ]
                    if 8 * q < QUARTER:
                        keep = (lane & (QUARTER - 1)) <= sub + 8 * q
                        tiles = jnp.where(keep, low, 0.0), jnp.where(keep, high, low), jnp.where(keep, 0.0, high)
                    else:
                        tiles = low, high
                    for k, tile in enumerate(tiles):
                        parts.setdefault(k, []).append(tile)
                for k, pair in parts.items():
                    top = k * LANE + block * 16
                    bands[group, top : top + 16, quad * LANE : (quad + 1) * LANE] = jnp.concatenate(
                        pair, axis=0
                    ).astype(jnp.bfloat16)
        return carry

    steps = groups // 4
    early = jnp.where(my_tmpl == 0, steps, jnp.where(my_tmpl * 2 < peers, steps // 2, 0))
    ahead = my_tmpl * 2 < peers
    pl.when(ahead)(prepare)
    lax.fori_loop(0, early, build, 0)

    for target in range(1, peers):
        @pl.when(target > my_tmpl)
        def _():
            pl.semaphore_wait(ready.at[target - 1], 1)
            block_to(target).start()

    @pl.when(my_tmpl == 0)
    def _():
        pl.semaphore_wait(barrier, owners - 1)
        for step in range(1, owners):
            pl.semaphore_signal(
                relay, inc=1, device_id={"sta": lax.rem(my_sta + step, owners)}, device_id_type=MESH
            )
        pl.semaphore_wait(relay, owners - 1)
        for target in range(1, peers):
            pl.semaphore_signal(relay, inc=1, device_id={"tmpl": target}, device_id_type=MESH)

    pl.when(jnp.logical_not(ahead))(prepare)
    middle = jnp.maximum(early, steps * 3 // 6)
    lax.fori_loop(early, middle, build, 0)

    @pl.when(last & patient)
    def _():
        for target in range(1, peers - 1):
            block_to(target).start()

    lax.fori_loop(middle, steps, build, 0)

    pltpu.make_async_copy(gathered, gathered, data_recv).wait()
    for c in range(channels):
        whole = jnp.concatenate([gathered[i, c] for i in range(peers)], axis=1)
        shifted = [whole] + [
            jnp.concatenate([whole[:, k * QUARTER :], whole[:, : k * QUARTER]], axis=1) for k in range(1, 4)
        ]
        for j in range(samples // LANE):
            rows = pl.ds(c * ROWS + j, stations, stride=channels * ROWS)
            for k in range(4):
                chunked[k, rows, :] = shifted[k][:, j * LANE : (j + 1) * LANE]

    def windows(which, group):
        return jnp.concatenate(
            [chunked[which, group * ROWS + i : group * ROWS + i + CHUNKS, :] for i in range(3)], axis=1
        )

    squares = []
    for group in range(groups):
        samples_in = windows(0, group)
        squares.append(samples_in * samples_in)
    squares = jnp.concatenate(squares, axis=0).astype(jnp.bfloat16)
    offset = lax.broadcasted_iota(jnp.int32, (BAND, LANE), 0) - lax.broadcasted_iota(
        jnp.int32, (BAND, LANE), 1
    )
    ones = jnp.where((offset >= 0) & (offset < TLEN), 1.0, 0.0).astype(jnp.bfloat16)
    energy = jnp.dot(squares, ones, preferred_element_type=jnp.float32)
    inverse[...] = lax.rsqrt(energy / TLEN + EPS)

    def correlate(group):
        stacked = jnp.concatenate([windows(k, group) for k in range(4)], axis=0).astype(jnp.bfloat16)
        raw = jnp.dot(stacked[:, : TLEN + QUARTER], bands[group], preferred_element_type=jnp.float32)
        local = inverse[group * CHUNKS : (group + 1) * CHUNKS, :]
        for quad in range(per_group // 4):
            part = [raw[k * CHUNKS : (k + 1) * CHUNKS, quad * LANE : (quad + 1) * LANE] for k in range(4)]
            for upper in range(2):
                near, far = [
                    jnp.where(left, pltpu.roll(part[k], HALF, 1), part[k + 2])
                    if upper
                    else jnp.where(left, part[k], pltpu.roll(part[k + 2], HALF, 1))
                    for k in range(2)
                ]
                for k, value in enumerate((
                    jnp.where(even_quarter, near, pltpu.roll(far, QUARTER, 1)),
                    jnp.where(even_quarter, pltpu.roll(near, LANE - QUARTER, 1), far),
                )):
                    row = group * per_group + 4 * quad + 2 * upper + k
                    lagged[row, 1 : CHUNKS + 1, :] = value * (local * norms[row : row + 1, :])

    zero = jnp.zeros((CHUNKS, LANE), jnp.float32)
    same, following = [zero] * per_group, [zero] * per_group

    def align(group):
        for t in range(per_group):
            row = group * per_group + t
            turn = turns[row]
            moved = pltpu.roll(lagged[row, pl.ds(chunks[row], CHUNKS), :], turn, 1)
            keep = lane < turn
            same[t] = same[t] + jnp.where(keep, moved, 0.0)
            following[t] = following[t] + jnp.where(keep, 0.0, moved)

    behind = 1
    for group in range(groups + behind):
        if group < groups:
            correlate(group)
        if group >= behind:
            align(group - behind)
    rows = LAGS // LANE
    for t in range(per_group):
        partial_ref[:, t, :] = same[t][:rows] + following[t][1 : rows + 1]

    span = LAGS // LANE // owners
    @pl.when(my_tmpl > 0)
    def _():
        pl.semaphore_wait(relay, 1)
    for step in range(owners - 1):
        target = step + jnp.where(my_sta <= step, 1, 0)
        pltpu.make_async_remote_copy(
            src_ref=partial_ref.at[pl.ds(target * span, span)],
            dst_ref=arrived.at[lax.rem(my_sta + owners - target, owners) - 1],
            send_sem=sum_sent,
            recv_sem=sum_recv,
            device_id={"sta": target},
            device_id_type=MESH,
        ).start()
    total = partial_ref[pl.ds(my_sta * span, span)]
    pltpu.make_async_copy(arrived, arrived, sum_recv).wait()
    for step in range(owners - 1):
        total = total + arrived[step]
    for i in range(span):
        out_ref[:, i * LANE : (i + 1) * LANE] = total[i]
    pltpu.make_async_copy(arrived, arrived, sum_sent).wait()
    others = gathered.at[pl.ds(0, peers - 1)]
    pltpu.make_async_copy(others, others, send_sem).wait()


def shards(data, templates, starts):
    peers, owners = lax.axis_size("tmpl"), lax.axis_size("sta")
    stations, channels, width = data.shape
    per_group = templates.shape[2]
    groups = stations * channels
    vmem = pl.BlockSpec(memory_space=pltpu.VMEM)
    span = LAGS // LANE // owners
    return pl.pallas_call(
        functools.partial(kernel, peers, owners),
        out_shape=jax.ShapeDtypeStruct((per_group, LAGS // owners), jnp.float32),
        in_specs=[pl.BlockSpec(memory_space=pltpu.HBM)] * 3,
        out_specs=vmem,
        scratch_shapes=[
            pltpu.SMEM((channels, per_group, stations), jnp.int32),
            pltpu.VMEM(templates.shape, templates.dtype),
            pltpu.SemaphoreType.DMA((2,)),
            pltpu.VMEM((peers, channels, stations, width), jnp.float32),
            pltpu.VMEM((4, groups * ROWS, LANE), jnp.float32),
            pltpu.VMEM((groups * per_group, TLEN), jnp.float32),
            pltpu.VMEM((groups, TLEN + QUARTER, per_group * QUARTER), jnp.bfloat16),
            pltpu.VMEM((groups * per_group, LANE), jnp.float32),
            pltpu.VMEM((groups * CHUNKS, LANE), jnp.float32),
            pltpu.VMEM((groups * per_group, ROWS, LANE), jnp.float32),
            pltpu.VMEM((LAGS // LANE, per_group, LANE), jnp.float32),
            pltpu.VMEM((owners - 1, span, per_group, LANE), jnp.float32),
            pltpu.SMEM((groups * per_group,), jnp.int32),
            pltpu.SMEM((groups * per_group,), jnp.int32),
            pltpu.SemaphoreType.DMA,
            pltpu.SemaphoreType.DMA,
            pltpu.SemaphoreType.DMA,
            pltpu.SemaphoreType.DMA,
            pltpu.SemaphoreType.REGULAR((peers - 1,)),
            pltpu.SemaphoreType.REGULAR,
        ],
        compiler_params=pltpu.CompilerParams(
            collective_id=0, has_side_effects=True, vmem_limit_bytes=64 * 1024 * 1024 - 10559488
        ),
    )(jnp.transpose(starts, (1, 2, 0)), jnp.transpose(data, (1, 0, 2)), templates)


def solution(mesh):
    return jax.shard_map(
        shards,
        mesh=mesh,
        in_specs=(
            P(("parts", "sta"), None, "tmpl"),
            P("sta", None, "tmpl", None),
            P("sta", None, "tmpl"),
        ),
        out_specs=P(("parts", "tmpl"), "sta"),
        check_vma=False,
    )
```

```python
import functools

import jax
import jax.numpy as jnp
from jax import lax
from jax.experimental import pallas as pl
from jax.experimental.pallas import tpu as pltpu
from jax.sharding import PartitionSpec as P

TLEN = 256
MAXSHIFT = 512
LAGS = 512
EXTENT = LAGS + MAXSHIFT
LANE = 128
CHUNKS = EXTENT // LANE
HALF = LANE // 2
QUARTER = LANE // 4
BAND = TLEN + LANE
ROWS = 16
EPS = 1e-06

MESH = pl.DeviceIdType.MESH


def kernel(
    peers, owners,
    starts_hbm, data_ref, templates_hbm, out_ref,
    starts_ref, templates_ref, local_sems, gathered, chunked, flat, bands, norms, inverse, lagged, partial_ref, arrived,
    turns, chunks,
    data_recv, send_sem, sum_sent, sum_recv, ready, relay,
):
    channels, stations, width = data_ref.shape
    per_group = templates_ref.shape[2]
    groups = stations * channels
    samples = width * peers
    my_tmpl = lax.axis_index("tmpl")
    my_sta = lax.axis_index("sta")

    last = my_tmpl == peers - 1
    lead = peers - 1
    side = jnp.where(last, 1, 0)
    patient = lax.rem(my_sta, 2) == 1
    barrier = pltpu.get_barrier_semaphore()

    def block_to(target):
        return pltpu.make_async_remote_copy(
            src_ref=data_ref,
            dst_ref=gathered.at[my_tmpl],
            send_sem=send_sem,
            recv_sem=data_recv.at[side],
            device_id={"tmpl": target},
            device_id_type=MESH,
        )

    @pl.when(last)
    def _():
        pl.semaphore_wait(barrier, peers - 1)
        block_to(0).start()
        for target in range(peers - 1):
            pl.semaphore_signal(ready.at[peers - 2], inc=1, device_id={"tmpl": target}, device_id_type=MESH)

        @pl.when(jnp.logical_not(patient))
        def _():
            for target in range(1, peers - 1):
                block_to(target).start()

    fetches = [
        pltpu.make_async_copy(templates_hbm, templates_ref, local_sems.at[0]),
        pltpu.make_async_copy(starts_hbm, starts_ref, local_sems.at[1]),
        pltpu.make_async_copy(data_ref, gathered.at[my_tmpl], data_recv.at[side]),
    ]
    for copy in fetches:
        copy.start()

    @pl.when(jnp.logical_not(last))
    def _():
        for step in range(1, peers):
            @pl.when(my_tmpl + step < peers)
            def _():
                pl.semaphore_signal(
                    barrier, inc=1, device_id={"tmpl": my_tmpl + step}, device_id_type=MESH
                )

        @pl.when(my_tmpl == 0)
        def _():
            for step in range(1, owners):
                pl.semaphore_signal(
                    barrier, inc=1, device_id={"sta": lax.rem(my_sta + step, owners)}, device_id_type=MESH
                )

        @pl.when(my_tmpl > 0)
        def _():
            pl.semaphore_wait(barrier, my_tmpl)
            for target in range(peers - 2):
                @pl.when(target < my_tmpl)
                def _():
                    block_to(target).start()
                    pl.semaphore_signal(
                        ready.at[my_tmpl - 1], inc=1, device_id={"tmpl": target}, device_id_type=MESH
                    )

    def prepare():
        fetches[0].wait()
        fetches[1].wait()
        for s in range(stations):
            for c in range(channels):
                row = (s * channels + c) * per_group
                flat[row : row + per_group, :] = templates_ref[s, c].astype(jnp.float32)
        waves = flat[...]
        tnorm = jnp.sum(waves * waves, axis=1, keepdims=True)
        norms[...] = jnp.broadcast_to(lax.rsqrt(tnorm / TLEN + EPS) / TLEN, norms.shape)
        down = lax.broadcasted_iota(jnp.int32, (TLEN, TLEN), 0)
        across = lax.broadcasted_iota(jnp.int32, (TLEN, TLEN), 1)
        flip = jnp.where(down + across == TLEN - 1, 1.0, 0.0).astype(jnp.bfloat16)
        flat[...] = jnp.dot(waves.astype(jnp.bfloat16), flip, preferred_element_type=jnp.float32)
        for row in range(groups * per_group):
            s, c, t = row // (channels * per_group), row // per_group % channels, row % per_group
            start = starts_ref[c, t, s]
            turns[row] = (0 - start) & (LANE - 1)
            chunks[row] = (start + LANE - 1) >> 7

    sub = lax.broadcasted_iota(jnp.int32, (8, LANE), 0)
    lane = lax.broadcasted_iota(jnp.int32, (8, LANE), 1)

    left = lane < HALF
    even_quarter = (lane & QUARTER) == 0

    def build(step, carry):
        for quad in range(per_group):
            group, quad = step * 4 + quad // (per_group // 4), quad % (per_group // 4)
            rows = []
            for k in range(4):
                row = flat[pl.ds(group * per_group + 4 * quad + k, 1), :]
                rows.append(
                    [jnp.broadcast_to(row[:, LANE:], (8, LANE)), jnp.broadcast_to(row[:, :LANE], (8, LANE))]
                )
            for block in range(LANE // 16):
                parts = {}
                for q in (2 * block, 2 * block + 1):
                    turned = [
                        [
                            pltpu.roll(x, (8 * q + QUARTER * k + 1) % LANE, 1, stride=1, stride_axis=0)
                            for x in rows[k]
                        ]
                        for k in range(4)
                    ]
                    low, high = [
                        jnp.where(
                            left,
                            jnp.where(even_quarter, turned[0][i], turned[1][i]),
                            jnp.where(even_quarter, turned[2][i], turned[3][i]),
                        )
                        for i in range(2)
                    ]
                    if 8 * q < QUARTER:
                        keep = (lane & (QUARTER - 1)) <= sub + 8 * q
                        tiles = jnp.where(keep, low, 0.0), jnp.where(keep, high, low), jnp.where(keep, 0.0, high)
                    else:
                        tiles = low, high
                    for k, tile in enumerate(tiles):
                        parts.setdefault(k, []).append(tile)
                for k, pair in parts.items():
                    top = k * LANE + block * 16
                    bands[group, top : top + 16, quad * LANE : (quad + 1) * LANE] = jnp.concatenate(
                        pair, axis=0
                    ).astype(jnp.bfloat16)
        return carry

    steps = groups // 4
    early = jnp.where(my_tmpl == 0, steps, jnp.where(my_tmpl * 2 < peers, steps // 2, 0))
    ahead = my_tmpl * 2 < peers
    pl.when(ahead)(prepare)
    lax.fori_loop(0, early, build, 0)

    for target in range(1, peers):
        @pl.when(target > my_tmpl)
        def _():
            pl.semaphore_wait(ready.at[target - 1], 1)
            block_to(target).start()

    @pl.when(my_tmpl == 0)
    def _():
        pl.semaphore_wait(barrier, owners - 1)
        for step in range(1, owners):
            pl.semaphore_signal(
                relay, inc=1, device_id={"sta": lax.rem(my_sta + step, owners)}, device_id_type=MESH
            )
        pl.semaphore_wait(relay, owners - 1)
        for target in range(1, peers):
            pl.semaphore_signal(relay, inc=1, device_id={"tmpl": target}, device_id_type=MESH)

    pl.when(jnp.logical_not(ahead))(prepare)
    middle = jnp.maximum(early, steps * 3 // 6)
    lax.fori_loop(early, middle, build, 0)

    @pl.when(last & patient)
    def _():
        for target in range(1, peers - 1):
            block_to(target).start()

    lax.fori_loop(middle, steps, build, 0)

    def spread(blocks, early):
        for c in range(channels):
            whole = jnp.concatenate([gathered[i, c] for i in range(blocks)], axis=1)
            for k in range(4):
                shifted = whole[:, k * QUARTER :]
                if not early and k:
                    shifted = jnp.concatenate([shifted, whole[:, : k * QUARTER]], axis=1)
                for j in range(samples // LANE):
                    if ((j + 1) * LANE + k * QUARTER <= lead * width) == early:
                        rows = pl.ds(c * ROWS + j, stations, stride=channels * ROWS)
                        chunked[k, rows, :] = shifted[:, j * LANE : (j + 1) * LANE]

    for which, part in enumerate((pl.ds(0, lead), pl.ds(lead, 1))):
        blocks = gathered.at[part]
        pltpu.make_async_copy(blocks, blocks, data_recv.at[which]).wait()
        spread(lead + which, which == 0)

    def windows(which, group):
        return jnp.concatenate(
            [chunked[which, group * ROWS + i : group * ROWS + i + CHUNKS, :] for i in range(3)], axis=1
        )

    squares = []
    for group in range(groups):
        samples_in = windows(0, group)
        squares.append(samples_in * samples_in)
    squares = jnp.concatenate(squares, axis=0).astype(jnp.bfloat16)
    offset = lax.broadcasted_iota(jnp.int32, (BAND, LANE), 0) - lax.broadcasted_iota(
        jnp.int32, (BAND, LANE), 1
    )
    ones = jnp.where((offset >= 0) & (offset < TLEN), 1.0, 0.0).astype(jnp.bfloat16)
    energy = jnp.dot(squares, ones, preferred_element_type=jnp.float32)
    inverse[...] = lax.rsqrt(energy / TLEN + EPS)

    def correlate(group):
        stacked = jnp.concatenate([windows(k, group) for k in range(4)], axis=0).astype(jnp.bfloat16)
        raw = jnp.dot(stacked[:, : TLEN + QUARTER], bands[group], preferred_element_type=jnp.float32)
        local = inverse[group * CHUNKS : (group + 1) * CHUNKS, :]
        for quad in range(per_group // 4):
            part = [raw[k * CHUNKS : (k + 1) * CHUNKS, quad * LANE : (quad + 1) * LANE] for k in range(4)]
            for upper in range(2):
                near, far = [
                    jnp.where(left, pltpu.roll(part[k], HALF, 1), part[k + 2])
                    if upper
                    else jnp.where(left, part[k], pltpu.roll(part[k + 2], HALF, 1))
                    for k in range(2)
                ]
                for k, value in enumerate((
                    jnp.where(even_quarter, near, pltpu.roll(far, QUARTER, 1)),
                    jnp.where(even_quarter, pltpu.roll(near, LANE - QUARTER, 1), far),
                )):
                    row = group * per_group + 4 * quad + 2 * upper + k
                    lagged[row, 1 : CHUNKS + 1, :] = value * (local * norms[row : row + 1, :])

    zero = jnp.zeros((CHUNKS, LANE), jnp.float32)
    same, following = [zero] * per_group, [zero] * per_group

    def align(group):
        for t in range(per_group):
            row = group * per_group + t
            turn = turns[row]
            moved = pltpu.roll(lagged[row, pl.ds(chunks[row], CHUNKS), :], turn, 1)
            keep = lane < turn
            same[t] = same[t] + jnp.where(keep, moved, 0.0)
            following[t] = following[t] + jnp.where(keep, 0.0, moved)

    behind = 1
    for group in range(groups + behind):
        if group < groups:
            correlate(group)
        if group >= behind:
            align(group - behind)
    rows = LAGS // LANE
    for t in range(per_group):
        partial_ref[:, t, :] = same[t][:rows] + following[t][1 : rows + 1]

    span = LAGS // LANE // owners
    @pl.when(my_tmpl > 0)
    def _():
        pl.semaphore_wait(relay, 1)
    for step in range(owners - 1):
        target = step + jnp.where(my_sta <= step, 1, 0)
        pltpu.make_async_remote_copy(
            src_ref=partial_ref.at[pl.ds(target * span, span)],
            dst_ref=arrived.at[lax.rem(my_sta + owners - target, owners) - 1],
            send_sem=sum_sent,
            recv_sem=sum_recv,
            device_id={"sta": target},
            device_id_type=MESH,
        ).start()
    total = partial_ref[pl.ds(my_sta * span, span)]
    pltpu.make_async_copy(arrived, arrived, sum_recv).wait()
    for step in range(owners - 1):
        total = total + arrived[step]
    for i in range(span):
        out_ref[:, i * LANE : (i + 1) * LANE] = total[i]
    pltpu.make_async_copy(arrived, arrived, sum_sent).wait()
    others = gathered.at[pl.ds(0, peers - 1)]
    pltpu.make_async_copy(others, others, send_sem).wait()


def shards(data, templates, starts):
    peers, owners = lax.axis_size("tmpl"), lax.axis_size("sta")
    stations, channels, width = data.shape
    per_group = templates.shape[2]
    groups = stations * channels
    vmem = pl.BlockSpec(memory_space=pltpu.VMEM)
    span = LAGS // LANE // owners
    return pl.pallas_call(
        functools.partial(kernel, peers, owners),
        out_shape=jax.ShapeDtypeStruct((per_group, LAGS // owners), jnp.float32),
        in_specs=[pl.BlockSpec(memory_space=pltpu.HBM)] * 3,
        out_specs=vmem,
        scratch_shapes=[
            pltpu.SMEM((channels, per_group, stations), jnp.int32),
            pltpu.VMEM(templates.shape, templates.dtype),
            pltpu.SemaphoreType.DMA((2,)),
            pltpu.VMEM((peers, channels, stations, width), jnp.float32),
            pltpu.VMEM((4, groups * ROWS, LANE), jnp.float32),
            pltpu.VMEM((groups * per_group, TLEN), jnp.float32),
            pltpu.VMEM((groups, TLEN + QUARTER, per_group * QUARTER), jnp.bfloat16),
            pltpu.VMEM((groups * per_group, LANE), jnp.float32),
            pltpu.VMEM((groups * CHUNKS, LANE), jnp.float32),
            pltpu.VMEM((groups * per_group, ROWS, LANE), jnp.float32),
            pltpu.VMEM((LAGS // LANE, per_group, LANE), jnp.float32),
            pltpu.VMEM((owners - 1, span, per_group, LANE), jnp.float32),
            pltpu.SMEM((groups * per_group,), jnp.int32),
            pltpu.SMEM((groups * per_group,), jnp.int32),
            pltpu.SemaphoreType.DMA((2,)),
            pltpu.SemaphoreType.DMA,
            pltpu.SemaphoreType.DMA,
            pltpu.SemaphoreType.DMA,
            pltpu.SemaphoreType.REGULAR((peers - 1,)),
            pltpu.SemaphoreType.REGULAR,
        ],
        compiler_params=pltpu.CompilerParams(
            collective_id=0, has_side_effects=True, vmem_limit_bytes=64 * 1024 * 1024 - 10559488
        ),
    )(jnp.transpose(starts, (1, 2, 0)), jnp.transpose(data, (1, 0, 2)), templates)


def solution(mesh):
    return jax.shard_map(
        shards,
        mesh=mesh,
        in_specs=(
            P(("parts", "sta"), None, "tmpl"),
            P("sta", None, "tmpl", None),
            P("sta", None, "tmpl"),
        ),
        out_specs=P(("parts", "tmpl"), "sta"),
        check_vma=False,
    )
```

```python
import functools

import jax
import jax.numpy as jnp
from jax import lax
from jax.experimental import pallas as pl
from jax.experimental.pallas import tpu as pltpu
from jax.sharding import PartitionSpec as P

TLEN = 256
MAXSHIFT = 512
LAGS = 512
EXTENT = LAGS + MAXSHIFT
LANE = 128
CHUNKS = EXTENT // LANE
HALF = LANE // 2
QUARTER = LANE // 4
BAND = TLEN + LANE
ROWS = 16
EPS = 1e-06

MESH = pl.DeviceIdType.MESH


def kernel(
    peers, owners,
    starts_hbm, data_ref, templates_hbm, out_ref,
    starts_ref, templates_ref, local_sems, gathered, chunked, flat, bands, norms, inverse, lagged, partial_ref, arrived,
    turns, chunks,
    data_recv, send_sem, sum_sent, sum_recv, ready, relay,
):
    channels, stations, width = data_ref.shape
    per_group = templates_ref.shape[2]
    groups = stations * channels
    samples = width * peers
    my_tmpl = lax.axis_index("tmpl")
    my_sta = lax.axis_index("sta")

    last = my_tmpl == peers - 1
    lead = peers - 1
    side = jnp.where(last, 1, 0)
    patient = lax.rem(my_sta, 2) == 1
    barrier = pltpu.get_barrier_semaphore()

    def block_to(target):
        return pltpu.make_async_remote_copy(
            src_ref=data_ref,
            dst_ref=gathered.at[my_tmpl],
            send_sem=send_sem,
            recv_sem=data_recv.at[side],
            device_id={"tmpl": target},
            device_id_type=MESH,
        )

    @pl.when(last)
    def _():
        pl.semaphore_wait(barrier, peers - 1)
        block_to(0).start()
        for target in range(peers - 1):
            pl.semaphore_signal(ready.at[peers - 2], inc=1, device_id={"tmpl": target}, device_id_type=MESH)

        @pl.when(jnp.logical_not(patient))
        def _():
            for target in range(1, peers - 1):
                block_to(target).start()

    fetches = [
        pltpu.make_async_copy(templates_hbm, templates_ref, local_sems.at[0]),
        pltpu.make_async_copy(starts_hbm, starts_ref, local_sems.at[1]),
        pltpu.make_async_copy(data_ref, gathered.at[my_tmpl], data_recv.at[side]),
    ]
    for copy in fetches:
        copy.start()

    @pl.when(jnp.logical_not(last))
    def _():
        for step in range(1, peers):
            @pl.when(my_tmpl + step < peers)
            def _():
                pl.semaphore_signal(
                    barrier, inc=1, device_id={"tmpl": my_tmpl + step}, device_id_type=MESH
                )

        @pl.when(my_tmpl == 0)
        def _():
            for step in range(1, owners):
                pl.semaphore_signal(
                    barrier, inc=1, device_id={"sta": lax.rem(my_sta + step, owners)}, device_id_type=MESH
                )

        @pl.when(my_tmpl > 0)
        def _():
            pl.semaphore_wait(barrier, my_tmpl)
            for target in range(peers - 2):
                @pl.when(target < my_tmpl)
                def _():
                    block_to(target).start()
                    pl.semaphore_signal(
                        ready.at[my_tmpl - 1], inc=1, device_id={"tmpl": target}, device_id_type=MESH
                    )

    def prepare():
        fetches[0].wait()
        fetches[1].wait()
        for s in range(stations):
            for c in range(channels):
                row = (s * channels + c) * per_group
                flat[row : row + per_group, :] = templates_ref[s, c].astype(jnp.float32)
        waves = flat[...]
        tnorm = jnp.sum(waves * waves, axis=1, keepdims=True)
        norms[...] = jnp.broadcast_to(lax.rsqrt(tnorm / TLEN + EPS) / TLEN, norms.shape)
        down = lax.broadcasted_iota(jnp.int32, (TLEN, TLEN), 0)
        across = lax.broadcasted_iota(jnp.int32, (TLEN, TLEN), 1)
        flip = jnp.where(down + across == TLEN - 1, 1.0, 0.0).astype(jnp.bfloat16)
        flat[...] = jnp.dot(waves.astype(jnp.bfloat16), flip, preferred_element_type=jnp.float32)
        for row in range(groups * per_group):
            s, c, t = row // (channels * per_group), row // per_group % channels, row % per_group
            start = starts_ref[c, t, s]
            turns[row] = (0 - start) & (LANE - 1)
            chunks[row] = (start + LANE - 1) >> 7

    sub = lax.broadcasted_iota(jnp.int32, (8, LANE), 0)
    lane = lax.broadcasted_iota(jnp.int32, (8, LANE), 1)

    left = lane < HALF
    even_quarter = (lane & QUARTER) == 0

    def build(step, carry):
        for quad in range(per_group):
            group, quad = step * 4 + quad // (per_group // 4), quad % (per_group // 4)
            rows = []
            for k in range(4):
                row = flat[pl.ds(group * per_group + 4 * quad + k, 1), :]
                rows.append(
                    [jnp.broadcast_to(row[:, LANE:], (8, LANE)), jnp.broadcast_to(row[:, :LANE], (8, LANE))]
                )
            for block in range(LANE // 16):
                parts = {}
                for q in (2 * block, 2 * block + 1):
                    turned = [
                        [
                            pltpu.roll(x, (8 * q + QUARTER * k + 1) % LANE, 1, stride=1, stride_axis=0)
                            for x in rows[k]
                        ]
                        for k in range(4)
                    ]
                    low, high = [
                        jnp.where(
                            left,
                            jnp.where(even_quarter, turned[0][i], turned[1][i]),
                            jnp.where(even_quarter, turned[2][i], turned[3][i]),
                        )
                        for i in range(2)
                    ]
                    if 8 * q < QUARTER:
                        keep = (lane & (QUARTER - 1)) <= sub + 8 * q
                        tiles = jnp.where(keep, low, 0.0), jnp.where(keep, high, low), jnp.where(keep, 0.0, high)
                    else:
                        tiles = low, high
                    for k, tile in enumerate(tiles):
                        parts.setdefault(k, []).append(tile)
                for k, pair in parts.items():
                    top = k * LANE + block * 16
                    bands[group, top : top + 16, quad * LANE : (quad + 1) * LANE] = jnp.concatenate(
                        pair, axis=0
                    ).astype(jnp.bfloat16)
        return carry

    steps = groups // 4
    early = jnp.where(my_tmpl == 0, steps, jnp.where(my_tmpl * 2 < peers, steps // 2, 0))
    ahead = my_tmpl * 2 < peers
    pl.when(ahead)(prepare)
    lax.fori_loop(0, early, build, 0)

    for target in range(1, peers):
        @pl.when(target > my_tmpl)
        def _():
            pl.semaphore_wait(ready.at[target - 1], 1)
            block_to(target).start()

    @pl.when(my_tmpl == 0)
    def _():
        pl.semaphore_wait(barrier, owners - 1)
        for step in range(1, owners):
            pl.semaphore_signal(
                relay, inc=1, device_id={"sta": lax.rem(my_sta + step, owners)}, device_id_type=MESH
            )
        pl.semaphore_wait(relay, owners - 1)
        for target in range(1, peers):
            pl.semaphore_signal(relay, inc=1, device_id={"tmpl": target}, device_id_type=MESH)

    pl.when(jnp.logical_not(ahead))(prepare)
    middle = jnp.maximum(early, steps * 3 // 6)
    lax.fori_loop(early, middle, build, 0)

    @pl.when(last & patient)
    def _():
        for target in range(1, peers - 1):
            block_to(target).start()

    lax.fori_loop(middle, steps, build, 0)

    def spread(blocks, early):
        for c in range(channels):
            whole = jnp.concatenate([gathered[i, c] for i in range(blocks)], axis=1)
            for k in range(4):
                shifted = whole[:, k * QUARTER :]
                if not early and k:
                    shifted = jnp.concatenate([shifted, whole[:, : k * QUARTER]], axis=1)
                for j in range(samples // LANE):
                    if ((j + 1) * LANE + k * QUARTER <= lead * width) == early:
                        rows = pl.ds(c * ROWS + j, stations, stride=channels * ROWS)
                        chunked[k, rows, :] = shifted[:, j * LANE : (j + 1) * LANE]

    for which, part in enumerate((pl.ds(0, lead), pl.ds(lead, 1))):
        blocks = gathered.at[part]
        pltpu.make_async_copy(blocks, blocks, data_recv.at[which]).wait()
        spread(lead + which, which == 0)

    def windows(which, group):
        return jnp.concatenate(
            [chunked[which, group * ROWS + i : group * ROWS + i + CHUNKS, :] for i in range(3)], axis=1
        )

    squares = []
    for group in range(groups):
        samples_in = windows(0, group)
        squares.append(samples_in * samples_in)
    squares = jnp.concatenate(squares, axis=0)
    upper = squares.astype(jnp.bfloat16)
    lower = (squares - upper.astype(jnp.float32)).astype(jnp.bfloat16)
    offset = lax.broadcasted_iota(jnp.int32, (BAND, LANE), 0) - lax.broadcasted_iota(
        jnp.int32, (BAND, LANE), 1
    )
    ones = jnp.where((offset >= 0) & (offset < TLEN), 1.0, 0.0).astype(jnp.bfloat16)
    energy = jnp.dot(upper, ones, preferred_element_type=jnp.float32) + jnp.dot(
        lower, ones, preferred_element_type=jnp.float32
    )
    inverse[...] = lax.rsqrt(energy / TLEN + EPS)

    def correlate(group):
        stacked = jnp.concatenate([windows(k, group) for k in range(4)], axis=0).astype(jnp.bfloat16)
        raw = jnp.dot(stacked[:, : TLEN + QUARTER], bands[group], preferred_element_type=jnp.float32)
        local = inverse[group * CHUNKS : (group + 1) * CHUNKS, :]
        for quad in range(per_group // 4):
            part = [raw[k * CHUNKS : (k + 1) * CHUNKS, quad * LANE : (quad + 1) * LANE] for k in range(4)]
            for upper in range(2):
                near, far = [
                    jnp.where(left, pltpu.roll(part[k], HALF, 1), part[k + 2])
                    if upper
                    else jnp.where(left, part[k], pltpu.roll(part[k + 2], HALF, 1))
                    for k in range(2)
                ]
                for k, value in enumerate((
                    jnp.where(even_quarter, near, pltpu.roll(far, QUARTER, 1)),
                    jnp.where(even_quarter, pltpu.roll(near, LANE - QUARTER, 1), far),
                )):
                    row = group * per_group + 4 * quad + 2 * upper + k
                    lagged[row, 1 : CHUNKS + 1, :] = value * (local * norms[row : row + 1, :])

    zero = jnp.zeros((CHUNKS, LANE), jnp.float32)
    same, following = [zero] * per_group, [zero] * per_group

    def align(group):
        for t in range(per_group):
            row = group * per_group + t
            turn = turns[row]
            moved = pltpu.roll(lagged[row, pl.ds(chunks[row], CHUNKS), :], turn, 1)
            keep = lane < turn
            same[t] = same[t] + jnp.where(keep, moved, 0.0)
            following[t] = following[t] + jnp.where(keep, 0.0, moved)

    behind = 1
    for group in range(groups + behind):
        if group < groups:
            correlate(group)
        if group >= behind:
            align(group - behind)
    rows = LAGS // LANE
    for t in range(per_group):
        partial_ref[:, t, :] = same[t][:rows] + following[t][1 : rows + 1]

    span = LAGS // LANE // owners
    @pl.when(my_tmpl > 0)
    def _():
        pl.semaphore_wait(relay, 1)
    for step in range(owners - 1):
        target = step + jnp.where(my_sta <= step, 1, 0)
        pltpu.make_async_remote_copy(
            src_ref=partial_ref.at[pl.ds(target * span, span)],
            dst_ref=arrived.at[lax.rem(my_sta + owners - target, owners) - 1],
            send_sem=sum_sent,
            recv_sem=sum_recv,
            device_id={"sta": target},
            device_id_type=MESH,
        ).start()
    total = partial_ref[pl.ds(my_sta * span, span)]
    pltpu.make_async_copy(arrived, arrived, sum_recv).wait()
    for step in range(owners - 1):
        total = total + arrived[step]
    for i in range(span):
        out_ref[:, i * LANE : (i + 1) * LANE] = total[i]
    pltpu.make_async_copy(arrived, arrived, sum_sent).wait()
    others = gathered.at[pl.ds(0, peers - 1)]
    pltpu.make_async_copy(others, others, send_sem).wait()


def shards(data, templates, starts):
    peers, owners = lax.axis_size("tmpl"), lax.axis_size("sta")
    stations, channels, width = data.shape
    per_group = templates.shape[2]
    groups = stations * channels
    vmem = pl.BlockSpec(memory_space=pltpu.VMEM)
    span = LAGS // LANE // owners
    return pl.pallas_call(
        functools.partial(kernel, peers, owners),
        out_shape=jax.ShapeDtypeStruct((per_group, LAGS // owners), jnp.float32),
        in_specs=[pl.BlockSpec(memory_space=pltpu.HBM)] * 3,
        out_specs=vmem,
        scratch_shapes=[
            pltpu.SMEM((channels, per_group, stations), jnp.int32),
            pltpu.VMEM(templates.shape, templates.dtype),
            pltpu.SemaphoreType.DMA((2,)),
            pltpu.VMEM((peers, channels, stations, width), jnp.float32),
            pltpu.VMEM((4, groups * ROWS, LANE), jnp.float32),
            pltpu.VMEM((groups * per_group, TLEN), jnp.float32),
            pltpu.VMEM((groups, TLEN + QUARTER, per_group * QUARTER), jnp.bfloat16),
            pltpu.VMEM((groups * per_group, LANE), jnp.float32),
            pltpu.VMEM((groups * CHUNKS, LANE), jnp.float32),
            pltpu.VMEM((groups * per_group, ROWS, LANE), jnp.float32),
            pltpu.VMEM((LAGS // LANE, per_group, LANE), jnp.float32),
            pltpu.VMEM((owners - 1, span, per_group, LANE), jnp.float32),
            pltpu.SMEM((groups * per_group,), jnp.int32),
            pltpu.SMEM((groups * per_group,), jnp.int32),
            pltpu.SemaphoreType.DMA((2,)),
            pltpu.SemaphoreType.DMA,
            pltpu.SemaphoreType.DMA,
            pltpu.SemaphoreType.DMA,
            pltpu.SemaphoreType.REGULAR((peers - 1,)),
            pltpu.SemaphoreType.REGULAR,
        ],
        compiler_params=pltpu.CompilerParams(
            collective_id=0, has_side_effects=True, vmem_limit_bytes=64 * 1024 * 1024 - 10559488
        ),
    )(jnp.transpose(starts, (1, 2, 0)), jnp.transpose(data, (1, 0, 2)), templates)


def solution(mesh):
    return jax.shard_map(
        shards,
        mesh=mesh,
        in_specs=(
            P(("parts", "sta"), None, "tmpl"),
            P("sta", None, "tmpl", None),
            P("sta", None, "tmpl"),
        ),
        out_specs=P(("parts", "tmpl"), "sta"),
        check_vma=False,
    )
```
